32 devices in a mesh: dp: 16 (over z, y, x), tensor: 2 (over core).
Axes of the slice: x: 2, y: 2, z: 4, core: 2. Of those that a mesh axis runs over, the one named last changes fastest.
Arguments:
- resid: bfloat16 [64, 32, 8192], P('dp'), may hold values from -6 to 6
- norm_gain: float32 [8192], replicated, may hold values from 0.1 to 1.9
- w_value: bfloat16 [8192, 768], P('dp', 'tensor'), may hold values from -0.0625 to 0.0625
- d_value: bfloat16 [64, 32, 768], P('dp', None, 'tensor'), may hold values from -6 to 6
- rewards: bfloat16 [64], P('dp'), may hold values from 0 to 1
- lengths: int32 [16, 4], P('dp'), may hold values from 1 to 32, 96 in all within a row
Outputs:
- value: bfloat16 [64, 32, 768], P('dp', None, 'tensor')
- w_grad: bfloat16 [8192, 768], P('dp', 'tensor')
The draws below stay inside these ranges and needn't reach their ends.
Inputs may be any that keep to these rules, and one draw needn't show every extreme that they name: The 4 responses of each index of dp have lengths that sum to exactly 96.
All inputs are finite; a program needn't handle non-finite values.
Results may differ from the reference program's by a relative error of at most 0.0058.
Values may be sent and summed in bfloat16 or wider, within the bound.
A program may use at most 64 MiB of HBM per device.

```python
import math
import jax
import jax.numpy as jnp
import numpy as np
from jax import lax

D = 8192
HV = 768
RPD = 4
SLOTS = 32
GROUP = 16
ROWS_DP = 96
ROLL = 64
N_DP = 16


def with_spikes(values, own_key, source, target, shards_of, factor):
    def block_of(axis_at):
        return (jnp.arange(values.shape[axis_at]) // (values.shape[axis_at] // shards_of)).reshape((-1,) + (1,) * (values.ndim - 1 - axis_at))

    first = jax.random.permutation(own_key, shards_of)[block_of(target)]
    other_side = (block_of(target) + shards_of // 2) % shards_of
    return jnp.where((block_of(source) == first) | (block_of(source) == other_side), factor * values, values)


def level_of(rng, shape, cuts, smallest, high):
    def one(dim, blocks):
        draws = jax.random.uniform(jax.random.fold_in(jax.random.fold_in(rng, 6), dim), (blocks,), jnp.float32, smallest / len(cuts), high / len(cuts))
        return jnp.repeat(jnp.exp(draws), shape[dim] // blocks).reshape((-1,) + (1,) * (len(shape) - dim - 1))

    factor_of = one(*cuts[0])
    for cut in cuts[1:]:
        factor_of = factor_of * one(*cut)
    return factor_of


def length_profile(number_of, total, bound, slope):
    portions = [(1 << 20) // math.isqrt(standing ** slope) + 1 for standing in range(2, number_of + 1)]
    surplus, given = total - bound - (number_of - 1), [1] * (number_of - 1)
    while surplus > 0:
        candidates = [i for i in range(number_of - 1) if given[i] < bound]
        whole, budget = sum([portions[i] for i in candidates]), surplus
        for i in candidates:
            addition = min(bound - given[i], max(1, budget * portions[i] // whole), surplus)
            given[i] = given[i] + addition
            surplus = surplus - addition
    return np.array([bound] + given)


def ragged(rng, number_of, total, reach, skew):
    if number_of == 2:
        one = jax.random.randint(rng, (), max(1, total - reach), min(reach, total - 1) + 1)
        return jnp.stack([one, total - one])
    tallies = jnp.asarray(length_profile(number_of, total, reach, skew), jnp.int32)
    pairs = (number_of - 1) // 2
    giver, taker = tallies[1:1 + 2 * pairs:2], tallies[2:2 + 2 * pairs:2]
    slack = jnp.minimum(giver - 1, reach - taker)
    shifted = jax.random.randint(jax.random.fold_in(rng, 1), (pairs,), 0, 1 << 20) % (slack + 1)
    tallies = tallies.at[1:1 + 2 * pairs:2].set(giver - shifted).at[2:2 + 2 * pairs:2].set(taker + shifted)
    return tallies[jax.random.permutation(jax.random.fold_in(rng, 2), number_of)]


def scatter_about(rng, dims, scale, bound, split=(), held_as=jnp.bfloat16):
    level = level_of(rng, dims, split, -0.22, 0.18) if split else 1.0
    entries = jax.random.normal(rng, dims, jnp.float32) * scale * level
    return jnp.minimum(jnp.maximum(entries, -bound), bound).astype(held_as)


def noise_with(own_key, dims, spread, reach, pieces, heavy, held_as=jnp.bfloat16):
    drawn = spread * jax.random.normal(own_key, dims, jnp.float32)
    if pieces:
        drawn = drawn * level_of(own_key, dims, pieces, -0.22, 0.18)
    return jnp.clip(with_spikes(drawn, jax.random.fold_in(own_key, 3), *heavy), -reach, reach).astype(held_as)


def setup_inputs(seed: int = 0) -> dict:
    streams_of = jax.random.split(jax.random.key(seed), 7)
    resid = noise_with(streams_of[0], (ROLL, SLOTS, D), 1.0, 6.0, ((0, 16),), (0, 2, 16, 2.0))
    norm_gain = jnp.clip(1.0 + 0.18 * jax.random.normal(streams_of[1], (D,), jnp.float32), 0.1, 1.9)
    w_value = scatter_about(streams_of[2], (D, HV), D ** -0.5, 0.0625, ((0, 16), (1, 2)))
    d_value = scatter_about(streams_of[3], (ROLL, SLOTS, HV), 1.0, 6.0, ((0, 16), (2, 2)))
    rewards = jnp.clip(1.0 * jax.random.uniform(streams_of[4], (ROLL,), jnp.float32) ** level_of(streams_of[4], (ROLL,), ((0, 16),), -0.2, 0.2), 0.0, 1.0).astype(jnp.bfloat16)
    lengths = jax.vmap(lambda own: ragged(own, RPD, ROWS_DP, SLOTS, 0))(jax.random.split(streams_of[5], N_DP)).reshape((N_DP, RPD)).astype(jnp.int32)
    return {"resid": resid, "norm_gain": norm_gain, "w_value": w_value, "d_value": d_value, "rewards": rewards, "lengths": lengths}


def reference(resid, norm_gain, w_value, d_value, rewards, lengths):
    roll_len = lengths.reshape(ROLL).astype(jnp.int32)
    reward_grid = rewards.astype(jnp.float32).reshape(ROLL // GROUP, GROUP)
    group_mean = lax.optimization_barrier(jnp.mean(reward_grid, axis=1, keepdims=True))
    group_spread = jnp.sqrt(lax.optimization_barrier(jnp.mean((reward_grid - group_mean) ** 2, axis=1, keepdims=True)))
    advantage = ((reward_grid - group_mean) / jnp.maximum(group_spread, 0.25)).reshape(ROLL)
    coef_roll = -advantage / roll_len.astype(jnp.float32)
    live_grid = (jnp.arange(SLOTS, dtype=jnp.int32)[None, :] < roll_len[:, None]).astype(jnp.float32)
    block_count = ROLL // GROUP
    resid_blocks = resid.reshape(block_count, GROUP * SLOTS, D)
    dval_blocks = d_value.reshape(block_count, GROUP * SLOTS, HV)
    live_blocks = live_grid.reshape(block_count, GROUP * SLOTS)
    coef_blocks = jnp.repeat(coef_roll, SLOTS).reshape(block_count, GROUP * SLOTS)

    def step_block(running, inputs):
        resid_rows, dval_rows, live_mask, row_coef = inputs
        states = resid_rows.astype(jnp.float32)
        mean_sq = lax.optimization_barrier(jnp.mean(states * states, axis=-1, keepdims=True))
        normed = (states * lax.rsqrt(mean_sq + 1e-05) * norm_gain).astype(jnp.bfloat16)
        value_rows = (jnp.dot(normed, w_value, preferred_element_type=jnp.float32) * live_mask[:, None]).astype(jnp.bfloat16)
        dscaled = (dval_rows.astype(jnp.float32) * (row_coef * live_mask)[:, None]).astype(jnp.bfloat16)
        running = running + jnp.dot(normed.T, dscaled, preferred_element_type=jnp.float32)
        return (running, value_rows)
    start_grad = jnp.zeros((D, HV), jnp.float32)
    grad_total, value_blocks = lax.scan(step_block, start_grad, (resid_blocks, dval_blocks, live_blocks, coef_blocks))
    value = value_blocks.reshape(ROLL, SLOTS, HV)
    return (value, grad_total.astype(jnp.bfloat16))
```

```python
import functools

import jax
import jax.numpy as jnp
from jax import lax
from jax.experimental import pallas as pl
from jax.experimental.pallas import tpu as pltpu
from jax.sharding import PartitionSpec as P

GROUP = 16
MESH = pl.DeviceIdType.MESH
F32 = jnp.float32
BF16 = jnp.bfloat16


def each(low, high, body):
    if high - low <= 4:
        for i in range(low, high):
            body(i)
    else:
        lax.fori_loop(low, high, lambda i, c: (body(i), c)[1], 0)


def kernel(
    n, tensor, per_dp, slots, live,
    resid_ref, gain_ref, w_ref, dval_ref, rew_ref, len_ref,
    value_ref, grad_ref,
    rew_all, nbuf, nrecv, dall, pbuf, pacc, vone, vtwo_out, vtwo, gacc, wpad,
    r_send, r_recv, n_send, n_recv, f_send, f_recv,
    d_send, d_recv, g_send, a_send, a_recv, b_send, b_recv,
):
    plane = GROUP // per_dp
    layers = n // plane
    total, width = resid_ref.shape
    feats = w_ref.shape[0]
    block = nbuf.shape[2]
    sub = block // feats
    share = tensor if live % (16 * tensor) == 0 else 1
    part = live // share

    d = lax.axis_index("dp")
    t = lax.axis_index("tensor")
    z = d // plane
    p = d % plane

    def rows_of(core):
        if share == 1:
            return pl.ds(0, live)
        return pl.ds(pl.multiple_of(core * part, 16), part)

    barrier = pltpu.get_barrier_semaphore()

    def greet(k):
        pl.semaphore_signal(
            barrier, inc=1, device_id={"dp": (d + k) % n, "tensor": t}, device_id_type=MESH
        )

    each(1, n, greet)
    for s in range(1, tensor):
        pl.semaphore_signal(
            barrier, inc=1, device_id={"dp": d, "tensor": (t + s) % tensor}, device_id_type=MESH
        )

    rew_all[p] = jnp.zeros(rew_all.shape[1:], F32)
    rew_all[p, 0:1, 0:per_dp] = rew_ref[...].astype(F32)

    slot_lane = lax.broadcasted_iota(jnp.int32, (1, total), 1)
    roll_lane = slot_lane // slots
    place = slot_lane % slots
    len_lane = jnp.zeros((1, total), jnp.int32)
    off_lane = jnp.zeros((1, total), jnp.int32)
    offset = jnp.int32(0)
    for j in range(per_dp):
        len_lane = jnp.where(roll_lane == j, len_ref[0, j], len_lane)
        off_lane = jnp.where(roll_lane == j, offset, off_lane)
        offset = offset + len_ref[0, j]
    target = jnp.where(place < len_lane, off_lane + place, -1)
    packed_row = lax.broadcasted_iota(jnp.int32, (live, total), 0)
    pack = jnp.where(packed_row == target, 1.0, 0.0).astype(BF16)

    chunk = 512 if width % 512 == 0 else 128
    lanes_sum = jnp.zeros((total, 128), F32)
    for c in range(width // chunk):
        x = resid_ref[:, c * chunk:(c + 1) * chunk].astype(F32)
        x = x * x
        for k in range(chunk // 128):
            lanes_sum = lanes_sum + x[:, k * 128:(k + 1) * 128]
    mean_sq = jnp.sum(lanes_sum, axis=1, keepdims=True) / width
    inv = lax.rsqrt(mean_sq + 1e-05)

    if sub == 1:
        wpad[...] = w_ref[...]
    else:
        for k in range(sub):
            wpad[k * feats:(k + 1) * feats, :] = jnp.where(
                d % sub == k, w_ref[...].astype(F32), 0.0
            ).astype(BF16)

    pl.semaphore_wait(barrier, n - 1 + tensor - 1)

    def reward_copy(k, slot):
        return pltpu.make_async_remote_copy(
            src_ref=rew_all.at[slot], dst_ref=rew_all.at[slot],
            send_sem=r_send.at[k], recv_sem=r_recv.at[slot],
            device_id={"dp": z * plane + (p + k) % plane, "tensor": t}, device_id_type=MESH,
        )

    for k in range(1, plane):
        reward_copy(k, p).start()

    def norm_block(j):
        at = pl.ds(pl.multiple_of((j // sub) * block, 128), block)
        x = resid_ref[:, at].astype(F32)
        normed = (x * inv * gain_ref[:, at]).astype(BF16)
        return jnp.dot(pack, normed, preferred_element_type=F32).astype(BF16)

    def norm_copy(j, source):
        return pltpu.make_async_remote_copy(
            src_ref=nbuf.at[j, rows_of(t)], dst_ref=nrecv.at[source, rows_of(t)],
            send_sem=n_send.at[j], recv_sem=n_recv.at[source],
            device_id={"dp": j, "tensor": t}, device_id_type=MESH,
        )

    def dest(dz, k):
        return ((z + dz) % layers) * plane + (p + k) % plane

    def origin(dz, k):
        return ((z + layers - dz) % layers) * plane + (p + plane - k) % plane

    def fill(dz):
        for k in range(plane):
            j = dest(dz, k)
            nbuf[j] = norm_block(j)

    def send_group(dz):
        for k in range(plane):
            norm_copy(dest(dz, k), d).start()

    fill(layers - 1)
    send_group(layers - 1)

    for k in range(1, plane):
        reward_copy(k, (p + plane - k) % plane).wait_recv()
    lane3 = lax.broadcasted_iota(jnp.int32, rew_all.shape, 2)
    sub3 = lax.broadcasted_iota(jnp.int32, rew_all.shape, 1)
    real = (lane3 < per_dp) & (sub3 == 0)
    rewards = jnp.where(real, rew_all[...], 0.0)

    def total_of(x):
        return jnp.sum(jnp.sum(jnp.sum(x, axis=0), axis=0, keepdims=True), axis=1, keepdims=True)

    mean = total_of(rewards) / GROUP
    away = jnp.where(real, rewards - mean[None], 0.0)
    spread = jnp.sqrt(total_of(away * away) / GROUP)
    own = rew_all[p][0:1, :]
    adv = (own - mean) / jnp.maximum(spread, 0.25)
    lane1 = lax.broadcasted_iota(jnp.int32, (1, 128), 1)
    len_of = jnp.ones((1, 128), jnp.int32)
    for j in range(per_dp):
        len_of = jnp.where(lane1 == j, len_ref[0, j], len_of)
    coef = -adv / len_of.astype(F32)
    slot_row = lax.broadcasted_iota(jnp.int32, (total, 128), 0) // slots
    lane2 = lax.broadcasted_iota(jnp.int32, (total, 128), 1)
    coef_row = jnp.sum(jnp.where(slot_row == lane2, coef, 0.0), axis=1, keepdims=True)
    scaled = (dval_ref[...].astype(F32) * coef_row).astype(BF16)
    dall[d] = jnp.dot(pack, scaled, preferred_element_type=F32).astype(BF16)

    def far_copy(dz, source):
        return pltpu.make_async_remote_copy(
            src_ref=dall.at[source], dst_ref=dall.at[source],
            send_sem=d_send.at[dz], recv_sem=d_recv.at[source],
            device_id={"dp": dest(dz, 0), "tensor": t}, device_id_type=MESH,
        )

    def near_copy(k, source):
        return pltpu.make_async_remote_copy(
            src_ref=dall.at[source], dst_ref=dall.at[source],
            send_sem=g_send.at[k, source // plane], recv_sem=d_recv.at[source],
            device_id={"dp": dest(0, k), "tensor": t}, device_id_type=MESH,
        )

    def rest(i):
        fill(layers - 2 - i)
        send_group(layers - 2 - i)

    if layers > 2:
        fill(layers - 2)
        each(1, layers, lambda dz: far_copy(dz, d).start())
        for k in range(1, plane):
            near_copy(k, d).start()
        send_group(layers - 2)
        each(1, layers - 2, rest)

    for k in range(1, plane):
        j = dest(0, k)
        nbuf[j] = norm_block(j)
    nrecv[d] = norm_block(d)
    if layers <= 2:
        each(1, layers, lambda dz: far_copy(dz, d).start())
        for k in range(1, plane):
            near_copy(k, d).start()
    for k in range(1, plane):
        norm_copy(dest(0, k), d).start()

    def pass_on(i):
        source = origin(layers - i, 0)
        far_copy(1, source).wait_recv()
        for k in range(1, plane):
            near_copy(k, source).start()

    each(1, layers, pass_on)

    def swap_copy(s, source, core):
        return pltpu.make_async_remote_copy(
            src_ref=nrecv.at[source, rows_of(core)], dst_ref=nrecv.at[source, rows_of(core)],
            send_sem=f_send.at[s, source], recv_sem=f_recv.at[s, source],
            device_id={"dp": d, "tensor": (t + s) % tensor}, device_id_type=MESH,
        )

    def value_copy(k, layer, writer):
        return pltpu.make_async_remote_copy(
            src_ref=pbuf.at[layer * plane + (p + plane - k) % plane],
            dst_ref=vone.at[writer, layer],
            send_sem=a_send.at[k, layer], recv_sem=a_recv.at[writer, layer],
            device_id={"dp": z * plane + (p + plane - k) % plane, "tensor": t}, device_id_type=MESH,
        )

    def take_in(dz, first):
        for k in range(first, plane):
            source = origin(dz, k)
            norm_copy(source, source).wait_recv()
            if share > 1:
                for s in range(1, tensor):
                    swap_copy(s, source, t).start()

    def multiply(dz, first):
        layer = (z + layers - dz) % layers
        for k in list(range(1, plane)) + [0]:
            source = origin(dz, k)
            if k >= first and share > 1:
                for s in range(1, tensor):
                    swap_copy(s, source, (t + tensor - s) % tensor).wait_recv()
            product = jnp.dot(nrecv[source], wpad[...], preferred_element_type=F32)
            if k == 0:
                pacc[layer] = product
            else:
                pbuf[source] = product.astype(BF16)
        for k in range(1, plane):
            value_copy(k, layer, p).start()

    def stage(i):
        dz = layers - i
        take_in(dz, 0)
        multiply(dz, 0)

    each(1, layers, stage)
    take_in(0, 1)
    multiply(0, 1)

    def plane_sum(layer):
        result = pacc[layer]
        for k in range(1, plane):
            writer = (p + k) % plane
            value_copy(k, layer, writer).wait_recv()
            result = result + vone[writer, layer].astype(F32)
        return result

    def layer_copy(layer, writer):
        return pltpu.make_async_remote_copy(
            src_ref=vtwo_out.at[layer], dst_ref=vtwo.at[writer],
            send_sem=b_send.at[layer], recv_sem=b_recv.at[writer],
            device_id={"dp": layer * plane + p, "tensor": t}, device_id_type=MESH,
        )

    def along(i):
        layer = (z + i) % layers
        vtwo_out[layer] = plane_sum(layer).astype(BF16)

    def along_send(i):
        layer_copy((z + i) % layers, z).start()

    each(1, layers, along)
    pacc[z] = plane_sum(z)
    each(1, layers, along_send)

    for k in range(1, plane):
        near_copy(k, z * plane + (p + k) % plane).wait_recv()

    def far_wait(dz):
        for k in range(1, plane):
            near_copy(k, origin(dz, k)).wait_recv()

    each(1, layers, far_wait)

    def grad_group(layer):
        at = pl.ds(layer * plane, plane)
        a = nrecv[at].reshape(plane * live, block)
        b = dall[at].reshape(plane * live, dall.shape[2])
        part_sum = lax.dot_general(
            a, b, (((0,), (0,)), ((), ())), preferred_element_type=F32
        )
        if isinstance(layer, int) and layer == 0:
            gacc[...] = part_sum
        else:
            gacc[...] = gacc[...] + part_sum

    grad_group(0)
    each(1, layers, grad_group)
    if sub == 1:
        grad_ref[...] = gacc[...].astype(BF16)
    else:
        chosen = gacc[0:feats, :]
        for k in range(1, sub):
            chosen = jnp.where(d % sub == k, gacc[k * feats:(k + 1) * feats, :], chosen)
        grad_ref[...] = chosen.astype(BF16)

    def add_in(i):
        writer = (z + i) % layers
        layer_copy(writer, writer).wait_recv()
        pacc[z] = pacc[z] + vtwo[writer].astype(F32)

    each(1, layers, add_in)
    rows = pacc[z].astype(BF16)
    value_ref[...] = lax.dot_general(
        pack, rows, (((0,), (0,)), ((), ())), preferred_element_type=F32
    ).astype(BF16)

    for k in range(1, plane):
        reward_copy(k, p).wait_send()

    def left(dz):
        far_copy(dz, d).wait_send()
        for k in range(plane):
            norm_copy(dest(dz, k), d).wait_send()
        layer_copy((z + dz) % layers, z).wait_send()

    each(1, layers, left)
    for k in range(1, plane):
        norm_copy(dest(0, k), d).wait_send()

    def left_too(layer):
        for k in range(1, plane):
            near_copy(k, layer * plane + p).wait_send()
            value_copy(k, layer, p).wait_send()

    each(0, layers, left_too)
    if share > 1:
        def left_swap(dz):
            for k in range(plane):
                for s in range(1, tensor):
                    swap_copy(s, origin(dz, k), t).wait_send()

        each(1, layers, left_swap)
        for k in range(1, plane):
            for s in range(1, tensor):
                swap_copy(s, origin(0, k), t).wait_send()


def per_device(n, tensor, resid, norm_gain, w_value, d_value, rewards, lengths):
    per_dp, slots, width = resid.shape
    feats, cols = w_value.shape
    total = per_dp * slots
    live = total * 3 // 4
    plane = GROUP // per_dp
    layers = n // plane
    block = max(feats, 128)
    dma = pltpu.SemaphoreType.DMA
    vmem = pl.BlockSpec(memory_space=pltpu.VMEM)
    value, grad = pl.pallas_call(
        functools.partial(kernel, n, tensor, per_dp, slots, live),
        out_shape=(
            jax.ShapeDtypeStruct((total, cols), BF16),
            jax.ShapeDtypeStruct((feats, cols), BF16),
        ),
        in_specs=[vmem] * 5 + [pl.BlockSpec(memory_space=pltpu.SMEM)],
        out_specs=(vmem, vmem),
        scratch_shapes=[
            pltpu.VMEM((plane, 8, 128), F32),
            pltpu.VMEM((n, live, block), BF16),
            pltpu.VMEM((n, live, block), BF16),
            pltpu.VMEM((n, live, cols), BF16),
            pltpu.VMEM((n, live, cols), BF16),
            pltpu.VMEM((layers, live, cols), F32),
            pltpu.VMEM((plane, layers, live, cols), BF16),
            pltpu.VMEM((layers, live, cols), BF16),
            pltpu.VMEM((layers, live, cols), BF16),
            pltpu.VMEM((block, cols), F32),
            pltpu.VMEM((block, cols), BF16),
            dma((plane,)), dma((plane,)),
            dma((n,)), dma((n,)),
            dma((tensor, n)), dma((tensor, n)),
            dma((layers,)), dma((n,)),
            dma((plane, layers)),
            dma((plane, layers)), dma((plane, layers)),
            dma((layers,)), dma((layers,)),
        ],
        compiler_params=pltpu.CompilerParams(
            collective_id=0, has_side_effects=True, vmem_limit_bytes=56 * 1024 * 1024
        ),
    )(
        resid.reshape(total, width),
        norm_gain.reshape(1, width),
        w_value,
        d_value.reshape(total, cols),
        rewards.reshape(1, per_dp),
        lengths,
    )
    return value.reshape(per_dp, slots, cols), grad


def solution(mesh):
    n, tensor = mesh.shape["dp"], mesh.shape["tensor"]
    return jax.shard_map(
        functools.partial(per_device, n, tensor),
        mesh=mesh,
        in_specs=(
            P("dp", None, None),
            P(),
            P("dp", "tensor"),
            P("dp", None, "tensor"),
            P("dp"),
            P("dp", None),
        ),
        out_specs=(P("dp", None, "tensor"), P("dp", "tensor")),
        check_vma=False,
    )
```

```python
import functools

import jax
import jax.numpy as jnp
from jax import lax
from jax.experimental import pallas as pl
from jax.experimental.pallas import tpu as pltpu
from jax.sharding import PartitionSpec as P

GROUP = 16
MESH = pl.DeviceIdType.MESH
F32 = jnp.float32
BF16 = jnp.bfloat16


def each(low, high, body):
    if high - low <= 4:
        for i in range(low, high):
            body(i)
    else:
        lax.fori_loop(low, high, lambda i, c: (body(i), c)[1], 0)


def kernel(
    n, tensor, per_dp, slots, live,
    resid_hbm, gain_hbm, w_hbm, dval_hbm, rew_ref, len_ref,
    value_ref, grad_ref,
    resid_ref, gain_ref, w_ref, dval_ref,
    rew_all, nbuf, nrecv, dall, pbuf, pkeep, pacc, vdiag, vone, vtwo_out, vtwo, gacc, wpad,
    in_sem, r_send, r_recv, n_send, n_recv, f_send, f_recv,
    l_send, d_recv, g_send, h_send, c_send, c_recv, a_send, a_recv, b_send, b_recv,
):
    plane = GROUP // per_dp
    layers = n // plane
    total, width = resid_ref.shape
    feats = w_ref.shape[0]
    block = nbuf.shape[2]
    sub = block // feats
    share = tensor if live % (16 * tensor) == 0 else 1
    part = live // share

    d = lax.axis_index("dp")
    t = lax.axis_index("tensor")
    z = d // plane
    p = d % plane
    across, up = p % 2, p // 2
    peer = [p, up * 2 + 1 - across, (1 - up) * 2 + across, 3 - p]
    half = live // 2

    loads = [
        pltpu.make_async_copy(source, place, in_sem.at[k])
        for k, (source, place) in enumerate(
            ((resid_hbm, resid_ref), (gain_hbm, gain_ref), (w_hbm, w_ref), (dval_hbm, dval_ref))
        )
    ]

    def rows_of(core):
        if share == 1:
            return pl.ds(0, live)
        return pl.ds(pl.multiple_of(core * part, 16), part)

    barrier = pltpu.get_barrier_semaphore()

    def greet(k):
        pl.semaphore_signal(
            barrier, inc=1, device_id={"dp": (d + k) % n, "tensor": t}, device_id_type=MESH
        )

    each(1, n, greet)
    for s in range(1, tensor):
        pl.semaphore_signal(
            barrier, inc=1, device_id={"dp": d, "tensor": (t + s) % tensor}, device_id_type=MESH
        )

    for load in loads:
        load.start()

    rew_all[p] = jnp.zeros(rew_all.shape[1:], F32)
    rew_all[p, 0:1, 0:per_dp] = rew_ref[...].astype(F32)

    slot_lane = lax.broadcasted_iota(jnp.int32, (1, total), 1)
    roll_lane = slot_lane // slots
    place = slot_lane % slots
    len_lane = jnp.zeros((1, total), jnp.int32)
    off_lane = jnp.zeros((1, total), jnp.int32)
    offset = jnp.int32(0)
    for j in range(per_dp):
        len_lane = jnp.where(roll_lane == j, len_ref[0, j], len_lane)
        off_lane = jnp.where(roll_lane == j, offset, off_lane)
        offset = offset + len_ref[0, j]
    target = jnp.where(place < len_lane, off_lane + place, -1)
    packed_row = lax.broadcasted_iota(jnp.int32, (live, total), 0)
    pack = jnp.where(packed_row == target, 1.0, 0.0).astype(BF16)

    for load in loads:
        load.wait()

    chunk = 512 if width % 512 == 0 else 128
    lanes_sum = jnp.zeros((total, 128), F32)
    for c in range(width // chunk):
        x = resid_ref[:, c * chunk:(c + 1) * chunk].astype(F32)
        x = x * x
        for k in range(chunk // 128):
            lanes_sum = lanes_sum + x[:, k * 128:(k + 1) * 128]
    mean_sq = jnp.sum(lanes_sum, axis=1, keepdims=True) / width
    inv = lax.rsqrt(mean_sq + 1e-05)

    if sub == 1:
        wpad[...] = w_ref[...]
    else:
        for k in range(sub):
            wpad[k * feats:(k + 1) * feats, :] = jnp.where(
                d % sub == k, w_ref[...].astype(F32), 0.0
            ).astype(BF16)

    pl.semaphore_wait(barrier, n - 1 + tensor - 1)

    def reward_copy(k, slot):
        return pltpu.make_async_remote_copy(
            src_ref=rew_all.at[slot], dst_ref=rew_all.at[slot],
            send_sem=r_send.at[k], recv_sem=r_recv.at[slot],
            device_id={"dp": z * plane + peer[k], "tensor": t}, device_id_type=MESH,
        )

    for k in range(1, plane):
        reward_copy(k, p).start()

    def norm_block(j):
        at = pl.ds(pl.multiple_of((j // sub) * block, 128), block)
        x = resid_ref[:, at].astype(F32)
        normed = (x * inv * gain_ref[:, at]).astype(BF16)
        return jnp.dot(pack, normed, preferred_element_type=F32).astype(BF16)

    def norm_copy(j, source):
        return pltpu.make_async_remote_copy(
            src_ref=nbuf.at[j, rows_of(t)], dst_ref=nrecv.at[source, rows_of(t)],
            send_sem=n_send.at[j], recv_sem=n_recv.at[source],
            device_id={"dp": j, "tensor": t}, device_id_type=MESH,
        )

    def dest(dz, k):
        return ((z + dz) % layers) * plane + peer[k]

    def origin(dz, k):
        return ((z + layers - dz) % layers) * plane + peer[k]

    def fill(dz):
        for k in range(plane):
            j = dest(dz, k)
            nbuf[j] = norm_block(j)

    def send_group(dz):
        for k in range(plane):
            norm_copy(dest(dz, k), d).start()

    fill(layers - 1)
    send_group(layers - 1)

    for k in range(1, plane):
        reward_copy(k, peer[k]).wait_recv()
    lane3 = lax.broadcasted_iota(jnp.int32, rew_all.shape, 2)
    sub3 = lax.broadcasted_iota(jnp.int32, rew_all.shape, 1)
    real = (lane3 < per_dp) & (sub3 == 0)
    rewards = jnp.where(real, rew_all[...], 0.0)

    def total_of(x):
        return jnp.sum(jnp.sum(jnp.sum(x, axis=0), axis=0, keepdims=True), axis=1, keepdims=True)

    mean = total_of(rewards) / GROUP
    away = jnp.where(real, rewards - mean[None], 0.0)
    spread = jnp.sqrt(total_of(away * away) / GROUP)
    own = rew_all[p][0:1, :]
    adv = (own - mean) / jnp.maximum(spread, 0.25)
    lane1 = lax.broadcasted_iota(jnp.int32, (1, 128), 1)
    len_of = jnp.ones((1, 128), jnp.int32)
    for j in range(per_dp):
        len_of = jnp.where(lane1 == j, len_ref[0, j], len_of)
    coef = -adv / len_of.astype(F32)
    slot_row = lax.broadcasted_iota(jnp.int32, (total, 128), 0) // slots
    lane2 = lax.broadcasted_iota(jnp.int32, (total, 128), 1)
    coef_row = jnp.sum(jnp.where(slot_row == lane2, coef, 0.0), axis=1, keepdims=True)
    scaled = (dval_ref[...].astype(F32) * coef_row).astype(BF16)
    dall[d] = jnp.dot(pack, scaled, preferred_element_type=F32).astype(BF16)

    def line_copy(way, source):
        return pltpu.make_async_remote_copy(
            src_ref=dall.at[source], dst_ref=dall.at[source],
            send_sem=l_send.at[way, source // plane], recv_sem=d_recv.at[source, 0],
            device_id={"dp": ((z + (1, layers - 1)[way]) % layers) * plane + p, "tensor": t},
            device_id_type=MESH,
        )

    def near_copy(k, source):
        return pltpu.make_async_remote_copy(
            src_ref=dall.at[source], dst_ref=dall.at[source],
            send_sem=g_send.at[k, source // plane], recv_sem=d_recv.at[source, 0],
            device_id={"dp": dest(0, k), "tensor": t}, device_id_type=MESH,
        )

    def half_copy(h, source):
        rows = pl.ds(h * half, half)
        return pltpu.make_async_remote_copy(
            src_ref=dall.at[source, rows], dst_ref=dall.at[source, rows],
            send_sem=h_send.at[h, source // plane], recv_sem=d_recv.at[source, h],
            device_id={"dp": dest(0, 2 - h), "tensor": t}, device_id_type=MESH,
        )

    room = (z + 1 < layers, z > 0)

    def send_own():
        for way in range(2):
            @pl.when(room[way])
            def _():
                line_copy(way, d).start()
        near_copy(1, d).start()
        near_copy(2, d).start()

    def rest(i):
        fill(layers - 2 - i)
        send_group(layers - 2 - i)

    if layers > 2:
        fill(layers - 2)
        send_own()
        send_group(layers - 2)
        each(1, layers - 2, rest)

    for k in range(1, plane):
        j = dest(0, k)
        nbuf[j] = norm_block(j)
    nrecv[d] = norm_block(d)
    if layers <= 2:
        send_own()
    for k in range(1, plane):
        norm_copy(dest(0, k), d).start()

    def relay(h):
        for way in range(2):
            layer = z - h if way == 0 else z + h

            @pl.when((layer >= 0) & (layer < layers))
            def _():
                source = layer * plane + p
                line_copy(way, source).wait_recv()

                @pl.when(room[way])
                def _():
                    line_copy(way, source).start()

                near_copy(1, source).start()
                near_copy(2, source).start()

    def corner(layer):
        for h in range(2):
            source = layer * plane + peer[1 + h]
            near_copy(1 + h, source).wait_recv()
            half_copy(h, source).start()

    def swap_copy(s, source, core):
        return pltpu.make_async_remote_copy(
            src_ref=nrecv.at[source, rows_of(core)], dst_ref=nrecv.at[source, rows_of(core)],
            send_sem=f_send.at[s, source], recv_sem=f_recv.at[s, source],
            device_id={"dp": d, "tensor": (t + s) % tensor}, device_id_type=MESH,
        )

    def corner_value(h, layer):
        return pltpu.make_async_remote_copy(
            src_ref=pbuf.at[layer * plane + peer[3], pl.ds(h * half, half)],
            dst_ref=vdiag.at[h, layer],
            send_sem=c_send.at[h, layer], recv_sem=c_recv.at[h, layer],
            device_id={"dp": dest(0, 1 + h), "tensor": t}, device_id_type=MESH,
        )

    def value_copy(k, layer):
        return pltpu.make_async_remote_copy(
            src_ref=pbuf.at[layer * plane + peer[k]], dst_ref=vone.at[k - 1, layer],
            send_sem=a_send.at[k, layer], recv_sem=a_recv.at[k, layer],
            device_id={"dp": dest(0, k), "tensor": t}, device_id_type=MESH,
        )

    def take_in(dz, first):
        for k in range(first, plane):
            source = origin(dz, k)
            norm_copy(source, source).wait_recv()
            if share > 1:
                for s in range(1, tensor):
                    swap_copy(s, source, t).start()

    def multiply(dz, first):
        layer = (z + layers - dz) % layers
        for k in (3, 2, 1, 0):
            source = origin(dz, k)
            if k >= first and share > 1:
                for s in range(1, tensor):
                    swap_copy(s, source, (t + tensor - s) % tensor).wait_recv()
            product = jnp.dot(nrecv[source], wpad[...], preferred_element_type=F32)
            if k == 0:
                pacc[layer] = product
            else:
                pbuf[source] = product.astype(BF16)
            if k == 1:
                pkeep[1, layer] = product[half:, :]
            if k == 2:
                pkeep[0, layer] = product[:half, :]
        for h in range(2):
            corner_value(h, layer).start()

    def stage(i):
        dz = layers - i
        first = 1 if isinstance(dz, int) and dz == 0 else 0
        take_in(dz, first)
        multiply(dz, first)

    def merge(i):
        layer = (z + i) % layers
        for h in range(2):
            corner_value(h, layer).wait_recv()
            pbuf[layer * plane + peer[2 - h], pl.ds(h * half, half)] = (
                pkeep[h, layer] + vdiag[h, layer].astype(F32)
            ).astype(BF16)
        for k in (1, 2):
            value_copy(k, layer).start()

    def plane_sum(layer):
        result = pacc[layer]
        for k in (1, 2):
            value_copy(k, layer).wait_recv()
            result = result + vone[k - 1, layer].astype(F32)
        return result

    def layer_copy(layer, writer):
        return pltpu.make_async_remote_copy(
            src_ref=vtwo_out.at[layer], dst_ref=vtwo.at[writer],
            send_sem=b_send.at[layer], recv_sem=b_recv.at[writer],
            device_id={"dp": layer * plane + p, "tensor": t}, device_id_type=MESH,
        )

    def along(i):
        layer = (z + i) % layers
        vtwo_out[layer] = plane_sum(layer).astype(BF16)
        layer_copy(layer, z).start()

    if layers == 4:
        stage(1)
        relay(1)
        relay(2)
        stage(2)
        merge(1)
        relay(3)
        corner(z)
        stage(3)
        merge(2)
        along(1)
        stage(4)
        merge(3)
        along(2)
        merge(4)
        each(1, layers, lambda i: corner((z + i) % layers))
        along(3)
    else:
        each(1, layers, relay)
        each(0, layers, corner)
        each(1, layers, stage)
        stage(layers)
        each(1, layers + 1, merge)
        each(1, layers, along)
    pacc[z] = plane_sum(z)

    def corner_wait(layer):
        for h in range(2):
            half_copy(h, layer * plane + peer[3]).wait_recv()

    each(0, layers, corner_wait)

    def grad_group(layer):
        at = pl.ds(layer * plane, plane)
        a = nrecv[at].reshape(plane * live, block)
        b = dall[at].reshape(plane * live, dall.shape[2])
        part_sum = lax.dot_general(
            a, b, (((0,), (0,)), ((), ())), preferred_element_type=F32
        )
        if isinstance(layer, int) and layer == 0:
            gacc[...] = part_sum
        else:
            gacc[...] = gacc[...] + part_sum

    grad_group(0)
    each(1, layers, grad_group)
    if sub == 1:
        grad_ref[...] = gacc[...].astype(BF16)
    else:
        chosen = gacc[0:feats, :]
        for k in range(1, sub):
            chosen = jnp.where(d % sub == k, gacc[k * feats:(k + 1) * feats, :], chosen)
        grad_ref[...] = chosen.astype(BF16)

    def add_in(i):
        writer = (z + i) % layers
        layer_copy(writer, writer).wait_recv()
        pacc[z] = pacc[z] + vtwo[writer].astype(F32)

    each(1, layers, add_in)
    rows = pacc[z].astype(BF16)
    value_ref[...] = lax.dot_general(
        pack, rows, (((0,), (0,)), ((), ())), preferred_element_type=F32
    ).astype(BF16)

    for k in range(1, plane):
        reward_copy(k, p).wait_send()

    def left(dz):
        for k in range(plane):
            norm_copy(dest(dz, k), d).wait_send()
        layer_copy((z + dz) % layers, z).wait_send()

    each(1, layers, left)
    for k in range(1, plane):
        norm_copy(dest(0, k), d).wait_send()

    def left_too(layer):
        for k in (1, 2):
            near_copy(k, layer * plane + p).wait_send()
            value_copy(k, layer).wait_send()
        for h in range(2):
            half_copy(h, layer * plane + peer[1 + h]).wait_send()
            corner_value(h, layer).wait_send()
        for way in range(2):
            behind = (layer <= z) if way == 0 else (layer >= z)

            @pl.when(behind & room[way])
            def _():
                line_copy(way, layer * plane + p).wait_send()

    each(0, layers, left_too)
    if share > 1:
        def left_swap(dz):
            for k in range(plane):
                for s in range(1, tensor):
                    swap_copy(s, origin(dz, k), t).wait_send()

        each(1, layers, left_swap)
        for k in range(1, plane):
            for s in range(1, tensor):
                swap_copy(s, origin(0, k), t).wait_send()


def per_device(n, tensor, resid, norm_gain, w_value, d_value, rewards, lengths):
    per_dp, slots, width = resid.shape
    feats, cols = w_value.shape
    total = per_dp * slots
    live = total * 3 // 4
    plane = GROUP // per_dp
    layers = n // plane
    block = max(feats, 128)
    dma = pltpu.SemaphoreType.DMA
    vmem = pl.BlockSpec(memory_space=pltpu.VMEM)
    value, grad = pl.pallas_call(
        functools.partial(kernel, n, tensor, per_dp, slots, live),
        out_shape=(
            jax.ShapeDtypeStruct((total, cols), BF16),
            jax.ShapeDtypeStruct((feats, cols), BF16),
        ),
        in_specs=[pl.BlockSpec(memory_space=pltpu.HBM)] * 4 + [vmem] + [pl.BlockSpec(memory_space=pltpu.SMEM)],
        out_specs=(vmem, vmem),
        scratch_shapes=[
            pltpu.VMEM((total, width), BF16),
            pltpu.VMEM((1, width), F32),
            pltpu.VMEM((feats, cols), BF16),
            pltpu.VMEM((total, cols), BF16),
            pltpu.VMEM((plane, 8, 128), F32),
            pltpu.VMEM((n, live, block), BF16),
            pltpu.VMEM((n, live, block), BF16),
            pltpu.VMEM((n, live, cols), BF16),
            pltpu.VMEM((n, live, cols), BF16),
            pltpu.VMEM((2, layers, live // 2, cols), F32),
            pltpu.VMEM((layers, live, cols), F32),
            pltpu.VMEM((2, layers, live // 2, cols), BF16),
            pltpu.VMEM((2, layers, live, cols), BF16),
            pltpu.VMEM((layers, live, cols), BF16),
            pltpu.VMEM((layers, live, cols), BF16),
            pltpu.VMEM((block, cols), F32),
            pltpu.VMEM((block, cols), BF16),
            dma((4,)), dma((plane,)), dma((plane,)),
            dma((n,)), dma((n,)),
            dma((tensor, n)), dma((tensor, n)),
            dma((2, layers)), dma((n, 2)), dma((3, layers)), dma((2, layers)),
            dma((2, layers)), dma((2, layers)),
            dma((3, layers)), dma((3, layers)),
            dma((layers,)), dma((layers,)),
        ],
        compiler_params=pltpu.CompilerParams(
            collective_id=0, has_side_effects=True, vmem_limit_bytes=56 * 1024 * 1024
        ),
    )(
        resid.reshape(total, width),
        norm_gain.reshape(1, width),
        w_value,
        d_value.reshape(total, cols),
        rewards.reshape(1, per_dp),
        lengths,
    )
    return value.reshape(per_dp, slots, cols), grad


def solution(mesh):
    n, tensor = mesh.shape["dp"], mesh.shape["tensor"]
    return jax.shard_map(
        functools.partial(per_device, n, tensor),
        mesh=mesh,
        in_specs=(
            P("dp", None, None),
            P(),
            P("dp", "tensor"),
            P("dp", None, "tensor"),
            P("dp"),
            P("dp", None),
        ),
        out_specs=(P("dp", None, "tensor"), P("dp", "tensor")),
        check_vma=False,
    )
```

```python
import functools

import jax
import jax.numpy as jnp
from jax import lax
from jax.experimental import pallas as pl
from jax.experimental.pallas import tpu as pltpu
from jax.sharding import PartitionSpec as P

GROUP = 16
MESH = pl.DeviceIdType.MESH
F32 = jnp.float32
BF16 = jnp.bfloat16


def each(low, high, body):
    if high - low <= 4:
        for i in range(low, high):
            body(i)
    else:
        lax.fori_loop(low, high, lambda i, c: (body(i), c)[1], 0)


def kernel(
    n, tensor, per_dp, slots, live,
    resid_hbm, gain_hbm, w_hbm, dval_hbm, rew_ref, len_ref,
    value_ref, grad_ref,
    resid_ref, gain_ref, w_ref, dval_ref,
    rew_all, nbuf, nrecv, dall, pbuf, pkeep, pacc, vdiag, vone, vtwo_out, vtwo, gacc, wpad,
    in_sem, r_send, r_recv, n_send, n_recv, f_send, f_recv,
    l_send, d_recv, g_send, h_send, c_send, c_recv, a_send, a_recv, b_send, b_recv,
):
    plane = GROUP // per_dp
    layers = n // plane
    total, width = resid_ref.shape
    feats = w_ref.shape[0]
    block = nbuf.shape[2]
    sub = block // feats
    share = tensor if live % (16 * tensor) == 0 else 1
    part = live // share

    d = lax.axis_index("dp")
    t = lax.axis_index("tensor")
    z = d // plane
    p = d % plane
    across, up = p % 2, p // 2
    peer = [p, up * 2 + 1 - across, (1 - up) * 2 + across, 3 - p]
    half = live // 2

    loads = [
        pltpu.make_async_copy(source, place, in_sem.at[k])
        for k, (source, place) in enumerate(
            ((resid_hbm, resid_ref), (gain_hbm, gain_ref), (w_hbm, w_ref), (dval_hbm, dval_ref))
        )
    ]

    def rows_of(core):
        if share == 1:
            return pl.ds(0, live)
        return pl.ds(pl.multiple_of(core * part, 16), part)

    barrier = pltpu.get_barrier_semaphore()

    def greet(k):
        pl.semaphore_signal(
            barrier, inc=1, device_id={"dp": (d + k) % n, "tensor": t}, device_id_type=MESH
        )

    each(1, n, greet)
    for s in range(1, tensor):
        pl.semaphore_signal(
            barrier, inc=1, device_id={"dp": d, "tensor": (t + s) % tensor}, device_id_type=MESH
        )

    for load in loads:
        load.start()

    rew_all[p] = jnp.zeros(rew_all.shape[1:], F32)
    rew_all[p, 0:1, 0:per_dp] = rew_ref[...].astype(F32)

    slot_lane = lax.broadcasted_iota(jnp.int32, (1, total), 1)
    roll_lane = slot_lane // slots
    place = slot_lane % slots
    len_lane = jnp.zeros((1, total), jnp.int32)
    off_lane = jnp.zeros((1, total), jnp.int32)
    offset = jnp.int32(0)
    for j in range(per_dp):
        len_lane = jnp.where(roll_lane == j, len_ref[0, j], len_lane)
        off_lane = jnp.where(roll_lane == j, offset, off_lane)
        offset = offset + len_ref[0, j]
    target = jnp.where(place < len_lane, off_lane + place, -1)
    packed_row = lax.broadcasted_iota(jnp.int32, (live, total), 0)
    pack = jnp.where(packed_row == target, 1.0, 0.0).astype(BF16)

    for load in loads:
        load.wait()

    chunk = 512 if width % 512 == 0 else 128
    lanes_sum = jnp.zeros((total, 128), F32)
    for c in range(width // chunk):
        x = resid_ref[:, c * chunk:(c + 1) * chunk].astype(F32)
        x = x * x
        for k in range(chunk // 128):
            lanes_sum = lanes_sum + x[:, k * 128:(k + 1) * 128]
    mean_sq = jnp.sum(lanes_sum, axis=1, keepdims=True) / width
    inv = lax.rsqrt(mean_sq + 1e-05)

    if sub == 1:
        wpad[...] = w_ref[...]
    else:
        for k in range(sub):
            wpad[k * feats:(k + 1) * feats, :] = jnp.where(
                d % sub == k, w_ref[...].astype(F32), 0.0
            ).astype(BF16)

    pl.semaphore_wait(barrier, n - 1 + tensor - 1)

    def reward_copy(k, slot):
        return pltpu.make_async_remote_copy(
            src_ref=rew_all.at[slot], dst_ref=rew_all.at[slot],
            send_sem=r_send.at[k], recv_sem=r_recv.at[slot],
            device_id={"dp": z * plane + peer[k], "tensor": t}, device_id_type=MESH,
        )

    for k in range(1, plane):
        reward_copy(k, p).start()

    def norm_block(j):
        at = pl.ds(pl.multiple_of((j // sub) * block, 128), block)
        x = resid_ref[:, at].astype(F32)
        normed = (x * inv * gain_ref[:, at]).astype(BF16)
        return jnp.dot(pack, normed, preferred_element_type=F32).astype(BF16)

    def norm_copy(j, source):
        return pltpu.make_async_remote_copy(
            src_ref=nbuf.at[j, rows_of(t)], dst_ref=nrecv.at[source, rows_of(t)],
            send_sem=n_send.at[j], recv_sem=n_recv.at[source],
            device_id={"dp": j, "tensor": t}, device_id_type=MESH,
        )

    def dest(dz, k):
        return ((z + dz) % layers) * plane + peer[k]

    def origin(dz, k):
        return ((z + layers - dz) % layers) * plane + peer[k]

    def fill(dz):
        for k in range(plane):
            j = dest(dz, k)
            nbuf[j] = norm_block(j)

    def send_group(dz):
        for k in range(plane):
            norm_copy(dest(dz, k), d).start()

    for k in range(1, plane):
        j = dest(0, k)
        nbuf[j] = norm_block(j)
    nrecv[d] = norm_block(d)
    fill(layers - 1)
    for k in range(1, plane):
        norm_copy(dest(0, k), d).start()
    send_group(layers - 1)

    for k in range(1, plane):
        reward_copy(k, peer[k]).wait_recv()
    lane3 = lax.broadcasted_iota(jnp.int32, rew_all.shape, 2)
    sub3 = lax.broadcasted_iota(jnp.int32, rew_all.shape, 1)
    real = (lane3 < per_dp) & (sub3 == 0)
    rewards = jnp.where(real, rew_all[...], 0.0)

    def total_of(x):
        return jnp.sum(jnp.sum(jnp.sum(x, axis=0), axis=0, keepdims=True), axis=1, keepdims=True)

    mean = total_of(rewards) / GROUP
    away = jnp.where(real, rewards - mean[None], 0.0)
    spread = jnp.sqrt(total_of(away * away) / GROUP)
    own = rew_all[p][0:1, :]
    adv = (own - mean) / jnp.maximum(spread, 0.25)
    lane1 = lax.broadcasted_iota(jnp.int32, (1, 128), 1)
    len_of = jnp.ones((1, 128), jnp.int32)
    for j in range(per_dp):
        len_of = jnp.where(lane1 == j, len_ref[0, j], len_of)
    coef = -adv / len_of.astype(F32)
    slot_row = lax.broadcasted_iota(jnp.int32, (total, 128), 0) // slots
    lane2 = lax.broadcasted_iota(jnp.int32, (total, 128), 1)
    coef_row = jnp.sum(jnp.where(slot_row == lane2, coef, 0.0), axis=1, keepdims=True)
    scaled = (dval_ref[...].astype(F32) * coef_row).astype(BF16)
    dall[d] = jnp.dot(pack, scaled, preferred_element_type=F32).astype(BF16)

    def line_copy(way, source):
        return pltpu.make_async_remote_copy(
            src_ref=dall.at[source], dst_ref=dall.at[source],
            send_sem=l_send.at[way, source // plane], recv_sem=d_recv.at[source, 0],
            device_id={"dp": ((z + (1, layers - 1)[way]) % layers) * plane + p, "tensor": t},
            device_id_type=MESH,
        )

    def near_copy(k, source):
        return pltpu.make_async_remote_copy(
            src_ref=dall.at[source], dst_ref=dall.at[source],
            send_sem=g_send.at[k, source // plane], recv_sem=d_recv.at[source, 0],
            device_id={"dp": dest(0, k), "tensor": t}, device_id_type=MESH,
        )

    def half_copy(h, source):
        rows = pl.ds(h * half, half)
        return pltpu.make_async_remote_copy(
            src_ref=dall.at[source, rows], dst_ref=dall.at[source, rows],
            send_sem=h_send.at[h, source // plane], recv_sem=d_recv.at[source, h],
            device_id={"dp": dest(0, 2 - h), "tensor": t}, device_id_type=MESH,
        )

    room = (z + 1 < layers, z > 0)

    def send_own():
        for way in range(2):
            @pl.when(room[way])
            def _():
                line_copy(way, d).start()
        near_copy(1, d).start()
        near_copy(2, d).start()

    def rest(i):
        fill(layers - 2 - i)
        send_group(layers - 2 - i)

    fill(layers - 2)
    send_own()
    send_group(layers - 2)
    each(1, layers - 2, rest)

    def relay(h):
        for way in range(2):
            layer = z - h if way == 0 else z + h

            @pl.when((layer >= 0) & (layer < layers))
            def _():
                source = layer * plane + p
                line_copy(way, source).wait_recv()

                @pl.when(room[way])
                def _():
                    line_copy(way, source).start()

                near_copy(1, source).start()
                near_copy(2, source).start()

    def corner(layer):
        for h in range(2):
            source = layer * plane + peer[1 + h]
            near_copy(1 + h, source).wait_recv()
            half_copy(h, source).start()

    def swap_copy(s, source, core):
        return pltpu.make_async_remote_copy(
            src_ref=nrecv.at[source, rows_of(core)], dst_ref=nrecv.at[source, rows_of(core)],
            send_sem=f_send.at[s, source], recv_sem=f_recv.at[s, source],
            device_id={"dp": d, "tensor": (t + s) % tensor}, device_id_type=MESH,
        )

    def corner_value(h, layer):
        return pltpu.make_async_remote_copy(
            src_ref=pbuf.at[layer * plane + peer[3], pl.ds(h * half, half)],
            dst_ref=vdiag.at[h, layer],
            send_sem=c_send.at[h, layer], recv_sem=c_recv.at[h, layer],
            device_id={"dp": dest(0, 1 + h), "tensor": t}, device_id_type=MESH,
        )

    def value_copy(k, layer):
        return pltpu.make_async_remote_copy(
            src_ref=pbuf.at[layer * plane + peer[k]], dst_ref=vone.at[k - 1, layer],
            send_sem=a_send.at[k, layer], recv_sem=a_recv.at[k, layer],
            device_id={"dp": dest(0, k), "tensor": t}, device_id_type=MESH,
        )

    def take_in(dz, first):
        for k in range(first, plane):
            source = origin(dz, k)
            norm_copy(source, source).wait_recv()
            if share > 1:
                for s in range(1, tensor):
                    swap_copy(s, source, t).start()

    def multiply(dz, first):
        layer = (z + layers - dz) % layers
        for k in (3, 2, 1, 0):
            source = origin(dz, k)
            if k >= first and share > 1:
                for s in range(1, tensor):
                    swap_copy(s, source, (t + tensor - s) % tensor).wait_recv()
            product = jnp.dot(nrecv[source], wpad[...], preferred_element_type=F32)
            if k == 0:
                pacc[layer] = product
            else:
                pbuf[source] = product.astype(BF16)
            if k == 1:
                pkeep[1, layer] = product[half:, :]
            if k == 2:
                pkeep[0, layer] = product[:half, :]
        for h in range(2):
            corner_value(h, layer).start()

    def stage(i):
        dz = layers - i
        first = 1 if isinstance(dz, int) and dz == 0 else 0
        take_in(dz, first)
        multiply(dz, first)

    def merge(i):
        layer = (z + i) % layers
        for h in range(2):
            corner_value(h, layer).wait_recv()
            pbuf[layer * plane + peer[2 - h], pl.ds(h * half, half)] = (
                pkeep[h, layer] + vdiag[h, layer].astype(F32)
            ).astype(BF16)
        for k in (1, 2):
            value_copy(k, layer).start()

    def plane_sum(layer):
        result = pacc[layer]
        for k in (1, 2):
            value_copy(k, layer).wait_recv()
            result = result + vone[k - 1, layer].astype(F32)
        return result

    def layer_copy(layer, writer):
        return pltpu.make_async_remote_copy(
            src_ref=vtwo_out.at[layer], dst_ref=vtwo.at[writer],
            send_sem=b_send.at[layer], recv_sem=b_recv.at[writer],
            device_id={"dp": layer * plane + p, "tensor": t}, device_id_type=MESH,
        )

    def along(i):
        layer = (z + i) % layers
        vtwo_out[layer] = plane_sum(layer).astype(BF16)
        layer_copy(layer, z).start()

    if layers == 4:
        stage(4)
        relay(1)
        corner(z)
        stage(1)
        merge(4)
        relay(2)
        stage(2)
        merge(1)
        relay(3)
        stage(3)
        merge(2)
        along(1)
        each(1, layers, lambda i: corner((z + i) % layers))
        merge(3)
        along(2)
        along(3)
    else:
        each(1, layers, relay)
        each(0, layers, corner)
        each(1, layers, stage)
        stage(layers)
        each(1, layers + 1, merge)
        each(1, layers, along)
    pacc[z] = plane_sum(z)

    def corner_wait(layer):
        for h in range(2):
            half_copy(h, layer * plane + peer[3]).wait_recv()

    each(0, layers, corner_wait)

    def grad_group(layer):
        at = pl.ds(layer * plane, plane)
        a = nrecv[at].reshape(plane * live, block)
        b = dall[at].reshape(plane * live, dall.shape[2])
        part_sum = lax.dot_general(
            a, b, (((0,), (0,)), ((), ())), preferred_element_type=F32
        )
        if isinstance(layer, int) and layer == 0:
            gacc[...] = part_sum
        else:
            gacc[...] = gacc[...] + part_sum

    grad_group(0)
    each(1, layers, grad_group)
    if sub == 1:
        grad_ref[...] = gacc[...].astype(BF16)
    else:
        chosen = gacc[0:feats, :]
        for k in range(1, sub):
            chosen = jnp.where(d % sub == k, gacc[k * feats:(k + 1) * feats, :], chosen)
        grad_ref[...] = chosen.astype(BF16)

    def add_in(i):
        writer = (z + i) % layers
        layer_copy(writer, writer).wait_recv()
        pacc[z] = pacc[z] + vtwo[writer].astype(F32)

    each(1, layers, add_in)
    rows = pacc[z].astype(BF16)
    value_ref[...] = lax.dot_general(
        pack, rows, (((0,), (0,)), ((), ())), preferred_element_type=F32
    ).astype(BF16)

    for k in range(1, plane):
        reward_copy(k, p).wait_send()

    def left(dz):
        for k in range(plane):
            norm_copy(dest(dz, k), d).wait_send()
        layer_copy((z + dz) % layers, z).wait_send()

    each(1, layers, left)
    for k in range(1, plane):
        norm_copy(dest(0, k), d).wait_send()

    def left_too(layer):
        for k in (1, 2):
            near_copy(k, layer * plane + p).wait_send()
            value_copy(k, layer).wait_send()
        for h in range(2):
            half_copy(h, layer * plane + peer[1 + h]).wait_send()
            corner_value(h, layer).wait_send()
        for way in range(2):
            behind = (layer <= z) if way == 0 else (layer >= z)

            @pl.when(behind & room[way])
            def _():
                line_copy(way, layer * plane + p).wait_send()

    each(0, layers, left_too)
    if share > 1:
        def left_swap(dz):
            for k in range(plane):
                for s in range(1, tensor):
                    swap_copy(s, origin(dz, k), t).wait_send()

        each(1, layers, left_swap)
        for k in range(1, plane):
            for s in range(1, tensor):
                swap_copy(s, origin(0, k), t).wait_send()


def per_device(n, tensor, resid, norm_gain, w_value, d_value, rewards, lengths):
    per_dp, slots, width = resid.shape
    feats, cols = w_value.shape
    total = per_dp * slots
    live = total * 3 // 4
    plane = GROUP // per_dp
    layers = n // plane
    block = max(feats, 128)
    dma = pltpu.SemaphoreType.DMA
    vmem = pl.BlockSpec(memory_space=pltpu.VMEM)
    value, grad = pl.pallas_call(
        functools.partial(kernel, n, tensor, per_dp, slots, live),
        out_shape=(
            jax.ShapeDtypeStruct((total, cols), BF16),
            jax.ShapeDtypeStruct((feats, cols), BF16),
        ),
        in_specs=[pl.BlockSpec(memory_space=pltpu.HBM)] * 4 + [vmem] + [pl.BlockSpec(memory_space=pltpu.SMEM)],
        out_specs=(vmem, vmem),
        scratch_shapes=[
            pltpu.VMEM((total, width), BF16),
            pltpu.VMEM((1, width), F32),
            pltpu.VMEM((feats, cols), BF16),
            pltpu.VMEM((total, cols), BF16),
            pltpu.VMEM((plane, 8, 128), F32),
            pltpu.VMEM((n, live, block), BF16),
            pltpu.VMEM((n, live, block), BF16),
            pltpu.VMEM((n, live, cols), BF16),
            pltpu.VMEM((n, live, cols), BF16),
            pltpu.VMEM((2, layers, live // 2, cols), F32),
            pltpu.VMEM((layers, live, cols), F32),
            pltpu.VMEM((2, layers, live // 2, cols), BF16),
            pltpu.VMEM((2, layers, live, cols), BF16),
            pltpu.VMEM((layers, live, cols), BF16),
            pltpu.VMEM((layers, live, cols), BF16),
            pltpu.VMEM((block, cols), F32),
            pltpu.VMEM((block, cols), BF16),
            dma((4,)), dma((plane,)), dma((plane,)),
            dma((n,)), dma((n,)),
            dma((tensor, n)), dma((tensor, n)),
            dma((2, layers)), dma((n, 2)), dma((3, layers)), dma((2, layers)),
            dma((2, layers)), dma((2, layers)),
            dma((3, layers)), dma((3, layers)),
            dma((layers,)), dma((layers,)),
        ],
        compiler_params=pltpu.CompilerParams(
            collective_id=0, has_side_effects=True, vmem_limit_bytes=56 * 1024 * 1024
        ),
    )(
        resid.reshape(total, width),
        norm_gain.reshape(1, width),
        w_value,
        d_value.reshape(total, cols),
        rewards.reshape(1, per_dp),
        lengths,
    )
    return value.reshape(per_dp, slots, cols), grad


def solution(mesh):
    n, tensor = mesh.shape["dp"], mesh.shape["tensor"]
    return jax.shard_map(
        functools.partial(per_device, n, tensor),
        mesh=mesh,
        in_specs=(
            P("dp", None, None),
            P(),
            P("dp", "tensor"),
            P("dp", None, "tensor"),
            P("dp"),
            P("dp", None),
        ),
        out_specs=(P("dp", None, "tensor"), P("dp", "tensor")),
        check_vma=False,
    )
```
